512 devices in a mesh: dp: 4 (over x), row: 32 (over y, z_hi, core), col: 4 (over z_lo).
Axes of the slice: x: 4, y: 8, z: 8 (z_hi: 2, z_lo: 4; z = z_hi * 4 + z_lo), core: 2. Of those that a mesh axis runs over, the one named last changes fastest.
Arguments:
- tokens: bfloat16 [2048, 8192], P('dp', ('row', 'col')), may hold values from -6 to 6
- hidden_grad: bfloat16 [2048, 6656], P(('dp', 'row'), 'col'), may hold values from -6 to 6
- gate_weight: bfloat16 [8192, 6656], P('row', 'col'), may hold values from -0.0625 to 0.0625
- up_weight: bfloat16 [8192, 6656], P('row', 'col'), may hold values from -0.0625 to 0.0625
Outputs:
- input_grad: bfloat16 [2048, 8192], P('dp', ('row', 'col'))
- gate_grad: bfloat16 [8192, 6656], P('row', 'col')
- up_grad: bfloat16 [8192, 6656], P('row', 'col')
The draws below stay inside these ranges and needn't reach their ends.
All inputs are finite; a program needn't handle non-finite values.
Results may differ from the reference program's by a relative error of at most 0.022.
Values may be sent and summed in bfloat16 or wider, within the bound.
A program may use at most 64 MiB of HBM per device.

```python
import jax
import jax.numpy as jnp
from jax import lax

D = 8192
FF = 6656
TOKENS = 2048
N_ROW = 32


def level_of(own_key, extent, split, smallest, top_value):
    def one(axis_at, shards_of):
        steps = jax.random.uniform(jax.random.fold_in(jax.random.fold_in(own_key, 6), axis_at), (shards_of,), jnp.float32, smallest / len(split), top_value / len(split))
        return jnp.repeat(jnp.exp(steps), extent[axis_at] // shards_of).reshape((-1,) + (1,) * (len(extent) - axis_at - 1))

    gain = one(*split[0])
    for cut in split[1:]:
        gain = gain * one(*cut)
    return gain


def normal_values(key, dims, width, reach, cuts=(), kind=jnp.bfloat16):
    result = width * jax.random.normal(key, dims, jnp.float32)
    if cuts:
        result = result * level_of(key, dims, cuts, -0.22, 0.18)
    return jnp.clip(result, -reach, reach).astype(kind)


def setup_inputs(seed: int = 0) -> dict:
    key_list = jax.random.split(jax.random.key(seed), 5)
    tokens = normal_values(key_list[0], (TOKENS, D), 1.0, 6.0, ((0, 4), (1, 128)))
    hidden_grad = normal_values(key_list[1], (TOKENS, FF), 1.0, 6.0, ((0, 128), (1, 4)))
    gate_weight = normal_values(key_list[2], (D, FF), D ** -0.5, 0.0625, ((0, 32), (1, 4)))
    up_weight = normal_values(key_list[3], (D, FF), D ** -0.5, 0.0625, ((0, 32), (1, 4)))
    return {"tokens": tokens, "hidden_grad": hidden_grad, "gate_weight": gate_weight, "up_weight": up_weight}


def reference(tokens, hidden_grad, gate_weight, up_weight):
    block = D // N_ROW
    token_blocks = tokens.reshape(TOKENS, N_ROW, block).transpose(1, 0, 2)
    gate_blocks = gate_weight.reshape(N_ROW, block, FF)
    up_blocks = up_weight.reshape(N_ROW, block, FF)

    def add_block(carry, items):
        rows_in, gate_rows, up_rows = items
        gate_part = jnp.dot(rows_in, gate_rows, preferred_element_type=jnp.float32).astype(jnp.bfloat16)
        up_part = jnp.dot(rows_in, up_rows, preferred_element_type=jnp.float32).astype(jnp.bfloat16)
        gate_part, up_part = lax.optimization_barrier((gate_part, up_part))
        return (carry[0] + gate_part.astype(jnp.float32), carry[1] + up_part.astype(jnp.float32)), None

    zeros_init = jnp.zeros((TOKENS, FF), jnp.float32)
    (gate, up), _ = lax.scan(add_block, (zeros_init, zeros_init), (token_blocks, gate_blocks, up_blocks))
    sigma = jax.nn.sigmoid(gate)
    upstream = hidden_grad.astype(jnp.float32)
    gate_act_grad = (upstream * up * sigma * (1.0 + gate * (1.0 - sigma))).astype(jnp.bfloat16)
    up_act_grad = (upstream * gate * sigma).astype(jnp.bfloat16)
    input_grad = (jnp.dot(gate_act_grad, gate_weight.T, preferred_element_type=jnp.float32)
                  + jnp.dot(up_act_grad, up_weight.T, preferred_element_type=jnp.float32)).astype(jnp.bfloat16)
    gate_grad = jnp.dot(tokens.T, gate_act_grad, preferred_element_type=jnp.float32).astype(jnp.bfloat16)
    up_grad = jnp.dot(tokens.T, up_act_grad, preferred_element_type=jnp.float32).astype(jnp.bfloat16)
    return (input_grad, gate_grad, up_grad)
```

```python
import jax
import jax.numpy as jnp
from jax import lax
from jax.experimental import pallas as pl
from jax.experimental.pallas import tpu as pltpu
from jax.sharding import PartitionSpec as P

MESH = pl.DeviceIdType.MESH
F32 = jnp.float32
BF16 = jnp.bfloat16
NY, NX, NC = 8, 4, 4


def remote(src, dst, send, recv, target):
    copy = pltpu.make_async_remote_copy(
        src_ref=src,
        dst_ref=dst,
        send_sem=send,
        recv_sem=recv,
        device_id=target,
        device_id_type=MESH,
    )
    copy.start()
    return copy


def greet(targets):
    barrier = pltpu.get_barrier_semaphore()
    for target in targets:
        pl.semaphore_signal(barrier, inc=1, device_id=target, device_id_type=MESH)
    pl.semaphore_wait(barrier, len(targets))


def vmem():
    return pl.BlockSpec(memory_space=pltpu.VMEM)


def params(collective_id):
    return pltpu.CompilerParams(collective_id=collective_id, has_side_effects=True)


def gather_kernel(mine_ref, all_ref, local_sem, send_sem, recv_sem):
    col = lax.axis_index("col")
    peers = [{"col": lax.rem(col + o, NC)} for o in range(1, NC)]
    greet(peers)
    copies = [
        remote(mine_ref, all_ref.at[col], send_sem.at[o], recv_sem.at[o], peers[o])
        for o in range(NC - 1)
    ]
    own = pltpu.make_async_copy(mine_ref, all_ref.at[col], local_sem)
    own.start()
    own.wait()
    for copy in copies:
        copy.wait()


def gather_tokens(block):
    rows, tokens = block.shape
    return pl.pallas_call(
        gather_kernel,
        out_shape=jax.ShapeDtypeStruct((NC, rows, tokens), BF16),
        in_specs=[vmem()],
        out_specs=vmem(),
        scratch_shapes=[
            pltpu.SemaphoreType.DMA,
            pltpu.SemaphoreType.DMA((NC - 1,)),
            pltpu.SemaphoreType.DMA((NC - 1,)),
        ],
        compiler_params=params(0),
        name="gather_tokens",
    )(block)


def row_kernel(
    gate_ref, up_ref, hidden_ref, gate_out, up_out,
    core_in, ring_out, ring_in, own, pair_out, pair_in,
    core_send, core_recv, ring_send, ring_recv, pair_send, pair_recv,
    swap_send, swap_recv, turn_send, turn_recv, fwd_send, fwd_recv,
):
    row = lax.axis_index("row")
    y = lax.div(row, 4)
    core = lax.rem(row, 2)
    zh = lax.rem(lax.div(row, 2), 2)
    low = lax.rem(row, 4)
    ahead = {"row": lax.rem(y + 1, NY) * 4 + low}
    behind = {"row": lax.rem(y + NY - 1, NY) * 4 + low}
    partner = {"row": y * 4 + zh * 2 + (1 - core)}
    pair = {"row": y * 4 + (1 - zh) * 2 + core}
    greet([ahead, behind, partner, pair])

    ins = (gate_ref, up_ref)
    outs = (gate_out, up_out)
    nexts = (ahead, behind)
    zhs = (1 - zh, zh)

    def chunk(way, s):
        return lax.rem(y + NY - 1 - s, NY) if way == 0 else lax.rem(y + 1 + s, NY)

    started = []
    core_copies = {}
    for s in range(NY):
        for way in range(2):
            core_copies[way, s] = remote(
                ins[way].at[chunk(way, s), :, 1 - core],
                core_in.at[way, s],
                core_send.at[way, s],
                core_recv.at[way, s],
                partner,
            )
    ring_copies = {}
    pair_copies = []
    for s in range(NY):
        for way in range(2):
            core_copies[way, s].wait_recv()
        for j in range(2):
            for way in range(2):
                total = (
                    ins[way][chunk(way, s), zhs[j], core].astype(F32)
                    + core_in[way, s, zhs[j]].astype(F32)
                )
                if s > 0:
                    ring_copies[way, j, s - 1].wait_recv()
                    total = total + ring_in[way, j, s - 1].astype(F32)
                if s < NY - 1:
                    ring_out[way, j, s] = total.astype(BF16)
                    ring_copies[way, j, s] = remote(
                        ring_out.at[way, j, s],
                        ring_in.at[way, j, s],
                        ring_send.at[way, j, s],
                        ring_recv.at[way, j, s],
                        nexts[way],
                    )
                elif j == 0:
                    pair_out[way] = total.astype(BF16)
                    pair_copies.append(
                        remote(
                            pair_out.at[way],
                            pair_in.at[way],
                            pair_send.at[way],
                            pair_recv.at[way],
                            pair,
                        )
                    )
                else:
                    own[way] = total
    for copy in pair_copies:
        copy.wait_recv()
    gate = own[0] + pair_in[0].astype(F32)
    up = own[1] + pair_in[1].astype(F32)
    sigma = jax.nn.sigmoid(gate)
    upstream = hidden_ref[...].astype(F32)
    gate_out[y, zh, core] = (upstream * up * sigma * (1.0 + gate * (1.0 - sigma))).astype(BF16)
    up_out[y, zh, core] = (upstream * gate * sigma).astype(BF16)

    def place(way, j, s):
        at = lax.rem(y + NY - s, NY) if way == 0 else lax.rem(y + s, NY)
        return outs[way].at[at, zhs[j], core]

    swap_copies = [
        remote(place(way, 1, 0), place(way, 1, 0), swap_send.at[way], swap_recv.at[way], pair)
        for way in range(2)
    ]
    turn_copies = {}
    fwd_copies = {}

    def pass_on(way, j, s):
        here = place(way, j, s)
        if s < NY - 1:
            turn_copies[way, j, s] = remote(
                here, here, turn_send.at[way, j, s], turn_recv.at[way, j, s], nexts[way]
            )
        fwd_copies[way, j, s] = remote(
            here, here, fwd_send.at[way, j, s], fwd_recv.at[way, j, s], partner
        )

    late = 4
    for s in range(NY + late):
        if s < NY:
            for way in range(2):
                if s > 0:
                    turn_copies[way, 1, s - 1].wait_recv()
                pass_on(way, 1, s)
        if s >= late:
            for way in range(2):
                if s == late:
                    swap_copies[way].wait_recv()
                else:
                    turn_copies[way, 0, s - late - 1].wait_recv()
                pass_on(way, 0, s - late)
    for copy in fwd_copies.values():
        copy.wait_recv()
    for group in (core_copies, ring_copies, turn_copies, fwd_copies):
        started.extend(group.values())
    for copy in started + pair_copies + swap_copies:
        copy.wait_send()


def row_exchange(gate, up, hidden):
    rows, width = hidden.shape
    shape = (NY, 2, 2, rows, width)
    dma = pltpu.SemaphoreType.DMA
    gate_act, up_act = pl.pallas_call(
        row_kernel,
        out_shape=[jax.ShapeDtypeStruct(shape, BF16)] * 2,
        in_specs=[vmem()] * 3,
        out_specs=[vmem()] * 2,
        scratch_shapes=[
            pltpu.VMEM((2, NY, 2, rows, width), BF16),
            pltpu.VMEM((2, 2, NY - 1, rows, width), BF16),
            pltpu.VMEM((2, 2, NY - 1, rows, width), BF16),
            pltpu.VMEM((2, rows, width), F32),
            pltpu.VMEM((2, rows, width), BF16),
            pltpu.VMEM((2, rows, width), BF16),
            dma((2, NY)),
            dma((2, NY)),
            dma((2, 2, NY - 1)),
            dma((2, 2, NY - 1)),
            dma((2,)),
            dma((2,)),
            dma((2,)),
            dma((2,)),
            dma((2, 2, NY - 1)),
            dma((2, 2, NY - 1)),
            dma((2, 2, NY)),
            dma((2, 2, NY)),
        ],
        compiler_params=params(1),
        name="row_exchange",
    )(gate.reshape(shape), up.reshape(shape), hidden)
    return gate_act.reshape(-1, width), up_act.reshape(-1, width)


def sum_kernel(
    gate_ref, up_ref, input_ref, gate_out, up_out, input_out,
    ring_out, ring_in, peer_in,
    ring_send, ring_recv, turn_send, turn_recv, peer_send, peer_recv,
):
    dp = lax.axis_index("dp")
    col = lax.axis_index("col")
    nexts = ({"dp": lax.rem(dp + 1, NX)}, {"dp": lax.rem(dp + NX - 1, NX)})
    peers = [{"col": lax.rem(col + o, NC)} for o in range(1, NC)]
    greet([*nexts, *peers])
    ins = (gate_ref, up_ref)
    outs = (gate_out, up_out)

    def chunk(way, s):
        return lax.rem(dp + NX - 1 - s, NX) if way == 0 else lax.rem(dp + 1 + s, NX)

    ring_copies = {}
    turn_copies = {}
    peer_copies = []
    for s in range(NX):
        for j in range(2):
            for way in range(2):
                here = chunk(way, s)
                if s == 0:
                    ring_copies[way, j, s] = remote(
                        ins[way].at[here, j],
                        ring_in.at[way, j, s],
                        ring_send.at[way, j, s],
                        ring_recv.at[way, j, s],
                        nexts[way],
                    )
                    continue
                ring_copies[way, j, s - 1].wait_recv()
                total = ins[way][here, j].astype(F32) + ring_in[way, j, s - 1].astype(F32)
                if s < NX - 1:
                    ring_out[way, j, s - 1] = total.astype(BF16)
                    ring_copies[way, j, s] = remote(
                        ring_out.at[way, j, s - 1],
                        ring_in.at[way, j, s],
                        ring_send.at[way, j, s],
                        ring_recv.at[way, j, s],
                        nexts[way],
                    )
                else:
                    outs[way][here, j] = total.astype(BF16)
                    turn_copies[way, j, 0] = remote(
                        outs[way].at[here, j],
                        outs[way].at[here, j],
                        turn_send.at[way, j, 0],
                        turn_recv.at[way, j, 0],
                        nexts[way],
                    )
        if s == 0:
            for o in range(NC - 1):
                peer_copies.append(
                    remote(
                        input_ref.at[lax.rem(col + o + 1, NC)],
                        peer_in.at[o],
                        peer_send.at[o],
                        peer_recv.at[o],
                        peers[o],
                    )
                )
    for s in range(1, NX - 1):
        for j in range(2):
            for way in range(2):
                turn_copies[way, j, s - 1].wait_recv()
                at = lax.rem(dp + NX - s, NX) if way == 0 else lax.rem(dp + s, NX)
                turn_copies[way, j, s] = remote(
                    outs[way].at[at, j],
                    outs[way].at[at, j],
                    turn_send.at[way, j, s],
                    turn_recv.at[way, j, s],
                    nexts[way],
                )
    total = input_ref[col].astype(F32)
    for o in range(NC - 1):
        peer_copies[o].wait_recv()
        total = total + peer_in[o].astype(F32)
    input_out[...] = total.astype(BF16)
    for j in range(2):
        for way in range(2):
            turn_copies[way, j, NX - 2].wait_recv()
    for copy in [*ring_copies.values(), *turn_copies.values(), *peer_copies]:
        copy.wait_send()


def sum_grads(gate, up, share):
    features, width = gate.shape
    tokens = share.shape[1]
    half = features // NX // 2
    shape = (NX, 2, half, width)
    rows = features // NC
    dma = pltpu.SemaphoreType.DMA
    gate_sum, up_sum, input_sum = pl.pallas_call(
        sum_kernel,
        out_shape=[jax.ShapeDtypeStruct(shape, BF16)] * 2
        + [jax.ShapeDtypeStruct((rows, tokens), BF16)],
        in_specs=[vmem()] * 3,
        out_specs=[vmem()] * 3,
        scratch_shapes=[
            pltpu.VMEM((2, 2, NX - 2, half, width), BF16),
            pltpu.VMEM((2, 2, NX - 1, half, width), BF16),
            pltpu.VMEM((NC - 1, rows, tokens), BF16),
            dma((2, 2, NX - 1)),
            dma((2, 2, NX - 1)),
            dma((2, 2, NX - 1)),
            dma((2, 2, NX - 1)),
            dma((NC - 1,)),
            dma((NC - 1,)),
        ],
        compiler_params=params(2),
        name="sum_grads",
    )(gate.reshape(shape), up.reshape(shape), share.reshape(NC, rows, tokens))
    return gate_sum.reshape(features, width), up_sum.reshape(features, width), input_sum


def contract_rows(left, right):
    return lax.dot_general(left, right, (((0,), (0,)), ((), ())), preferred_element_type=F32)


def contract_cols(left, right):
    return lax.dot_general(left, right, (((1,), (1,)), ((), ())), preferred_element_type=F32)


def body(tokens, hidden_grad, gate_weight, up_weight):
    features = gate_weight.shape[0]
    panel_t = gather_tokens(tokens.T).reshape(features, -1)
    gate_act, up_act = row_exchange(
        contract_rows(panel_t, gate_weight).astype(BF16),
        contract_rows(panel_t, up_weight).astype(BF16),
        hidden_grad,
    )
    share = (contract_cols(gate_weight, gate_act) + contract_cols(up_weight, up_act)).astype(BF16)
    gate_local = jnp.dot(panel_t, gate_act, preferred_element_type=F32).astype(BF16)
    up_local = jnp.dot(panel_t, up_act, preferred_element_type=F32).astype(BF16)
    gate_sum, up_sum, input_sum = sum_grads(gate_local, up_local, share)
    return (input_sum.T, gate_sum, up_sum)


def solution(mesh):
    return jax.shard_map(
        body,
        mesh=mesh,
        in_specs=(
            P("dp", ("row", "col")),
            P(("dp", "row"), "col"),
            P("row", "col"),
            P("row", "col"),
        ),
        out_specs=(P("dp", ("row", "col")), P("row", "col"), P("row", "col")),
        check_vma=False,
    )
```

```python
import jax
import jax.numpy as jnp
from jax import lax
from jax.experimental import pallas as pl
from jax.experimental.pallas import tpu as pltpu
from jax.sharding import PartitionSpec as P

MESH = pl.DeviceIdType.MESH
F32 = jnp.float32
BF16 = jnp.bfloat16
NY, NX, NC = 8, 4, 4


def remote(src, dst, send, recv, target):
    copy = pltpu.make_async_remote_copy(
        src_ref=src,
        dst_ref=dst,
        send_sem=send,
        recv_sem=recv,
        device_id=target,
        device_id_type=MESH,
    )
    copy.start()
    return copy


def greet(targets):
    barrier = pltpu.get_barrier_semaphore()
    for target in targets:
        pl.semaphore_signal(barrier, inc=1, device_id=target, device_id_type=MESH)
    pl.semaphore_wait(barrier, len(targets))


def vmem():
    return pl.BlockSpec(memory_space=pltpu.VMEM)


def params(collective_id):
    return pltpu.CompilerParams(collective_id=collective_id, has_side_effects=True)


def gather_kernel(mine_ref, all_ref, local_sem, send_sem, recv_sem):
    col = lax.axis_index("col")
    peers = [{"col": lax.rem(col + o, NC)} for o in range(1, NC)]
    greet(peers)
    copies = [
        remote(mine_ref, all_ref.at[col], send_sem.at[o], recv_sem.at[o], peers[o])
        for o in range(NC - 1)
    ]
    own = pltpu.make_async_copy(mine_ref, all_ref.at[col], local_sem)
    own.start()
    own.wait()
    for copy in copies:
        copy.wait()


def gather_tokens(block):
    rows, tokens = block.shape
    return pl.pallas_call(
        gather_kernel,
        out_shape=jax.ShapeDtypeStruct((NC, rows, tokens), BF16),
        in_specs=[vmem()],
        out_specs=vmem(),
        scratch_shapes=[
            pltpu.SemaphoreType.DMA,
            pltpu.SemaphoreType.DMA((NC - 1,)),
            pltpu.SemaphoreType.DMA((NC - 1,)),
        ],
        compiler_params=params(0),
        name="gather_tokens",
    )(block)


def main_kernel(
    gate_ref, up_ref, hidden_ref, panel_ref, gate_weight_ref, up_weight_ref,
    gate_out, up_out, input_out,
    core_in, ring_out, ring_in, own, pair_out, pair_in, acts,
    local, dp_out, dp_in, share_out, share_in, share_own,
    core_send, core_recv, ring_send, ring_recv, pair_send, pair_recv,
    swap_send, swap_recv, turn_send, turn_recv, fwd_send, fwd_recv,
    dp_send, dp_recv, back_send, back_recv, share_send, share_recv,
):
    row = lax.axis_index("row")
    dp = lax.axis_index("dp")
    col = lax.axis_index("col")
    y = lax.div(row, 4)
    core = lax.rem(row, 2)
    zh = lax.rem(lax.div(row, 2), 2)
    low = lax.rem(row, 4)
    y_next = (
        {"row": lax.rem(y + 1, NY) * 4 + low},
        {"row": lax.rem(y + NY - 1, NY) * 4 + low},
    )
    x_next = ({"dp": lax.rem(dp + 1, NX)}, {"dp": lax.rem(dp + NX - 1, NX)})
    partner = {"row": y * 4 + zh * 2 + (1 - core)}
    pair = {"row": y * 4 + (1 - zh) * 2 + core}
    peers = [{"col": lax.rem(col + o, NC)} for o in range(1, NC)]
    greet([*y_next, partner, pair, *x_next, *peers])

    ins = (gate_ref, up_ref)
    outs = (gate_out, up_out)
    zhs = (1 - zh, zh)
    BOTH = ((0, 0), (0, 1), (1, 0), (1, 1))
    sent = []

    def send(*args):
        copy = remote(*args)
        sent.append(copy)
        return copy

    def hops(w, d):
        return NY // 2 if w == d else NY // 2 - 1

    def at_y(d, ahead):
        return lax.rem(y + NY + (ahead if d == 0 else -ahead), NY)

    MOST = NY // 2
    core_copies = {}
    for s in range(MOST):
        for w, d in BOTH:
            if s < hops(w, d):
                core_copies[w, d, s] = send(
                    ins[w].at[at_y(d, hops(w, d) - s), :, 1 - core],
                    core_in.at[w, d * MOST + s],
                    core_send.at[w, d * MOST + s],
                    core_recv.at[w, d * MOST + s],
                    partner,
                )
    for w in range(2):
        free = (1 - w) * MOST + MOST - 1
        core_copies[w] = send(
            ins[w].at[y, :, 1 - core],
            core_in.at[w, free],
            core_send.at[w, free],
            core_recv.at[w, free],
            partner,
        )
    ring = {}
    for s in range(MOST):
        for w, d in BOTH:
            if s >= hops(w, d):
                continue
            core_copies[w, d, s].wait_recv()
            for j in range(2):
                total = (
                    ins[w][at_y(d, hops(w, d) - s), zhs[j], core].astype(F32)
                    + core_in[w, d * MOST + s, zhs[j]].astype(F32)
                )
                if s > 0:
                    ring[w, d, j, s - 1].wait_recv()
                    total = total + ring_in[w, d, j, s - 1].astype(F32)
                ring_out[w, d, j, s] = total.astype(BF16)
                ring[w, d, j, s] = send(
                    ring_out.at[w, d, j, s],
                    ring_in.at[w, d, j, s],
                    ring_send.at[w, d, j, s],
                    ring_recv.at[w, d, j, s],
                    y_next[d],
                )
    for w in range(2):
        core_copies[w].wait_recv()
    pairs = []
    for j in range(2):
        for w in range(2):
            total = (
                ins[w][y, zhs[j], core].astype(F32)
                + core_in[w, (1 - w) * MOST + MOST - 1, zhs[j]].astype(F32)
            )
            for d in (1 - w, w):
                last = hops(w, d) - 1
                ring[w, d, j, last].wait_recv()
                total = total + ring_in[w, d, j, last].astype(F32)
            if j == 0:
                pair_out[w] = total.astype(BF16)
                pairs.append(
                    send(pair_out.at[w], pair_in.at[w], pair_send.at[w], pair_recv.at[w], pair)
                )
            else:
                own[w] = total
    for copy in pairs:
        copy.wait_recv()
    gate = own[0] + pair_in[0].astype(F32)
    up = own[1] + pair_in[1].astype(F32)
    sigma = jax.nn.sigmoid(gate)
    upstream = hidden_ref[...].astype(F32)
    acts[0, y, zh, core] = (upstream * up * sigma * (1.0 + gate * (1.0 - sigma))).astype(BF16)
    acts[1, y, zh, core] = (upstream * gate * sigma).astype(BF16)

    steps = []

    def plan(time, step, *args):
        steps.append((time, len(steps), step, args))

    turn = {}
    fwd = {}
    swap = [
        send(
            acts.at[w, y, zh, core], acts.at[w, y, zh, core], swap_send.at[w], swap_recv.at[w], pair
        )
        for w in range(2)
    ]

    def pass_on(w, d, j, s):
        here = acts.at[w, at_y(d, -s), zhs[j], core]
        if s > 0:
            turn[w, d, j, s - 1].wait_recv()
        if s < hops(w, d):
            turn[w, d, j, s] = send(
                here, here, turn_send.at[w, d, j, s], turn_recv.at[w, d, j, s], y_next[d]
            )
        if s > 0 or d == 0:
            fwd[w, d, j, s] = send(
                here, here, fwd_send.at[w, d, j, s], fwd_recv.at[w, d, j, s], partner
            )

    def arrive(w):
        swap[w].wait_recv()
        for d in range(2):
            pass_on(w, d, 0, 0)

    for w in range(2):
        for d in range(2):
            pass_on(w, d, 1, 0)
            for s in range(1, hops(w, d) + 1):
                plan(2.3 * s + 0.5 * w, pass_on, w, d, 1, s)
                plan((9.0, 13.0)[w] + 2.3 * s, pass_on, w, d, 0, s)
        plan((9.0, 13.0)[w], arrive, w)

    order = [lax.rem(dp + o, NX) for o in (NX - 1, 1, 2, 0)]
    slots = ((0, 2, 1, 3), (1, 2, 0, 3))
    half = local.shape[3]
    width = local.shape[4]
    dps = {}
    back = {}

    def gathered(w):
        for key, copy in fwd.items():
            if key[0] == w:
                copy.wait_recv()

    def dp_send_on(w, d, s, src):
        dps[w, d, s] = send(
            src, dp_in.at[w, d, s], dp_send.at[w, d, s], dp_recv.at[w, d, s], x_next[d]
        )

    def product(w, k):
        value = jnp.dot(
            panel_ref[order[k]],
            acts[w].reshape(-1, width),
            preferred_element_type=F32,
        ).astype(BF16)
        for d in range(2):
            local[w, k, d] = value[d * half : (d + 1) * half]
        if k < 2:
            dp_send_on(w, k, 0, local.at[w, k, k])

    def dp_step(w, d, s):
        dps[w, d, s - 1].wait_recv()
        total = local[w, slots[d][s], d].astype(F32) + dp_in[w, d, s - 1].astype(F32)
        if s < NX - 1:
            dp_out[w, d, s - 1] = total.astype(BF16)
            dp_send_on(w, d, s, dp_out.at[w, d, s - 1])
        else:
            outs[w][dp, d] = total.astype(BF16)
            back_on(w, d, 0)

    def back_on(w, d, s):
        if s > 0:
            back[w, d, s - 1].wait_recv()
        if s < NX - 1:
            at = lax.rem(dp + NX + (-s if d == 0 else s), NX)
            back[w, d, s] = send(
                outs[w].at[at, d],
                outs[w].at[at, d],
                back_send.at[w, d, s],
                back_recv.at[w, d, s],
                x_next[d],
            )

    starts = (20.0, 24.5)
    for w in range(2):
        plan(starts[w], gathered, w)
        for k in range(NX):
            plan(starts[w] + 0.1 + k, product, w, k)
        for d in range(2):
            for s in range(1, NX):
                plan(starts[w] + 1.5 + 4.8 * s, dp_step, w, d, s)
                plan(starts[w] + 1.5 + 4.8 * (NX - 1 + s), back_on, w, d, s)

    share = {}

    def share_step(o):
        block = lax.rem(col + o + 1, NC)
        total = lax.dot_general(
            gate_weight_ref[block], acts[0].reshape(-1, width), (((1,), (1,)), ((), ())),
            preferred_element_type=F32,
        ) + lax.dot_general(
            up_weight_ref[block], acts[1].reshape(-1, width), (((1,), (1,)), ((), ())),
            preferred_element_type=F32,
        )
        if o < NC - 1:
            share_out[o] = total.astype(BF16)
            share[o] = send(
                share_out.at[o], share_in.at[o], share_send.at[o], share_recv.at[o], peers[o]
            )
        else:
            share_own[...] = total

    def share_end():
        total = share_own[...]
        for o in range(NC - 1):
            share[o].wait_recv()
            total = total + share_in[o].astype(F32)
        input_out[...] = total.astype(BF16)

    for o in range(NC):
        plan(starts[1] + 5.0 + 2.4 * o, share_step, o)
    plan(starts[1] + 22.0, share_end)

    for _, _, step, args in sorted(steps, key=lambda item: item[:2]):
        step(*args)
    for copy in sent:
        copy.wait_send()


def main_call(gate, up, hidden, panel, gate_weight, up_weight):
    rows, width = hidden.shape
    features = gate_weight.shape[0]
    tokens = gate.shape[0]
    part = features // NC
    half = features // NX // 2
    shape = (NY, 2, 2, rows, width)
    most = NY // 2
    dma = pltpu.SemaphoreType.DMA
    vm = pltpu.VMEM
    gate_sum, up_sum, input_sum = pl.pallas_call(
        main_kernel,
        out_shape=[jax.ShapeDtypeStruct((NX, 2, half, width), BF16)] * 2
        + [jax.ShapeDtypeStruct((part, tokens), BF16)],
        in_specs=[vmem()] * 6,
        out_specs=[vmem()] * 3,
        scratch_shapes=[
            vm((2, 2 * most, 2, rows, width), BF16),
            vm((2, 2, 2, most, rows, width), BF16),
            vm((2, 2, 2, most, rows, width), BF16),
            vm((2, rows, width), F32),
            vm((2, rows, width), BF16),
            vm((2, rows, width), BF16),
            vm((2, *shape), BF16),
            vm((2, NX, 2, half, width), BF16),
            vm((2, 2, NX - 2, half, width), BF16),
            vm((2, 2, NX - 1, half, width), BF16),
            vm((NC - 1, part, tokens), BF16),
            vm((NC - 1, part, tokens), BF16),
            vm((part, tokens), F32),
            *[dma((2, 2 * most))] * 2,
            *[dma((2, 2, 2, most))] * 2,
            *[dma((2,))] * 2,
            *[dma((2,))] * 2,
            *[dma((2, 2, 2, most))] * 2,
            *[dma((2, 2, 2, most + 1))] * 2,
            *[dma((2, 2, NX - 1))] * 2,
            *[dma((2, 2, NX - 1))] * 2,
            *[dma((NC - 1,))] * 2,
        ],
        compiler_params=params(1),
        name="main",
    )(
        gate.reshape(shape),
        up.reshape(shape),
        hidden,
        panel.reshape(NX, features // NX, tokens),
        gate_weight.reshape(NC, part, width),
        up_weight.reshape(NC, part, width),
    )
    return input_sum.T, gate_sum.reshape(features, width), up_sum.reshape(features, width)


def contract_rows(left, right):
    return lax.dot_general(left, right, (((0,), (0,)), ((), ())), preferred_element_type=F32)


def body(tokens, hidden_grad, gate_weight, up_weight):
    features = gate_weight.shape[0]
    panel_t = gather_tokens(tokens.T).reshape(features, -1)
    return main_call(
        contract_rows(panel_t, gate_weight).astype(BF16),
        contract_rows(panel_t, up_weight).astype(BF16),
        hidden_grad,
        panel_t,
        gate_weight,
        up_weight,
    )


def solution(mesh):
    return jax.shard_map(
        body,
        mesh=mesh,
        in_specs=(
            P("dp", ("row", "col")),
            P(("dp", "row"), "col"),
            P("row", "col"),
            P("row", "col"),
        ),
        out_specs=(P("dp", ("row", "col")), P("row", "col"), P("row", "col")),
        check_vma=False,
    )
```

```python
import jax
import jax.numpy as jnp
from jax import lax
from jax.experimental import pallas as pl
from jax.experimental.pallas import tpu as pltpu
from jax.sharding import PartitionSpec as P

MESH = pl.DeviceIdType.MESH
F32 = jnp.float32
BF16 = jnp.bfloat16
NY, NX, NC = 8, 4, 4


def remote(src, dst, send, recv, target):
    copy = pltpu.make_async_remote_copy(
        src_ref=src,
        dst_ref=dst,
        send_sem=send,
        recv_sem=recv,
        device_id=target,
        device_id_type=MESH,
    )
    copy.start()
    return copy


def greet(targets):
    barrier = pltpu.get_barrier_semaphore()
    for target in targets:
        pl.semaphore_signal(barrier, inc=1, device_id=target, device_id_type=MESH)
    pl.semaphore_wait(barrier, len(targets))


def vmem():
    return pl.BlockSpec(memory_space=pltpu.VMEM)


def params(collective_id):
    return pltpu.CompilerParams(collective_id=collective_id, has_side_effects=True)


def main_kernel(
    tokens_ref, hidden_ref, gate_weight_ref, up_weight_ref,
    gate_out, up_out, input_out,
    panel_ref, panel_rows, parts, relay_in,
    core_in, ring_out, ring_in, own, pair_out, pair_in, acts,
    local, dp_out, dp_in, share_out, share_in, share_own,
    own_sem, panel_send, panel_recv, relay_send, relay_recv,
    core_send, core_recv, ring_send, ring_recv, pair_send, pair_recv,
    swap_send, swap_recv, turn_send, turn_recv, fwd_send, fwd_recv,
    dp_send, dp_recv, back_send, back_recv, share_send, share_recv,
):
    row = lax.axis_index("row")
    dp = lax.axis_index("dp")
    col = lax.axis_index("col")
    y = lax.div(row, 4)
    core = lax.rem(row, 2)
    zh = lax.rem(lax.div(row, 2), 2)
    low = lax.rem(row, 4)
    y_next = (
        {"row": lax.rem(y + 1, NY) * 4 + low},
        {"row": lax.rem(y + NY - 1, NY) * 4 + low},
    )
    x_next = ({"dp": lax.rem(dp + 1, NX)}, {"dp": lax.rem(dp + NX - 1, NX)})
    partner = {"row": y * 4 + zh * 2 + (1 - core)}
    z = zh * NC + col

    def at_z(hops):
        there = lax.rem(z + 2 * NC + hops, 2 * NC)
        return {"row": y * 4 + lax.div(there, NC) * 2 + core, "col": lax.rem(there, NC)}

    z_near = (at_z(-1), at_z(1))
    z_far = (at_z(-3), at_z(3))
    z_from = (lax.div(lax.rem(z + 1, 2 * NC), NC), lax.div(lax.rem(z + 2 * NC - 1, 2 * NC), NC))
    peers = [{"col": lax.rem(col + o, NC)} for o in range(1, NC)]
    greet([*y_next, partner, *z_near, *z_far, *x_next, *peers])

    weights = (gate_weight_ref, up_weight_ref)
    outs = (gate_out, up_out)
    zhs = (1 - zh, zh)
    BOTH = ((0, 0), (0, 1), (1, 0), (1, 1))
    sent = []

    def send(*args):
        copy = remote(*args)
        sent.append(copy)
        return copy

    def hops(w, d):
        return NY // 2 if w == d else NY // 2 - 1

    def at_y(d, ahead):
        return lax.rem(y + NY + (ahead if d == 0 else -ahead), NY)

    half = local.shape[3]
    width = local.shape[4]
    rows = hidden_ref.shape[0]
    panels = [
        send(tokens_ref, panel_ref.at[col], panel_send.at[o], panel_recv.at[o], peers[o])
        for o in range(NC - 1)
    ]
    mine = pltpu.make_async_copy(tokens_ref, panel_ref.at[col], own_sem)
    mine.start()
    mine.wait()
    for copy in panels:
        copy.wait_recv()
    panel_rows[...] = (
        panel_ref[...].reshape(-1, panel_ref.shape[2]).T.reshape(panel_rows.shape)
    )

    steps = []

    def plan(time, step, *args):
        steps.append((time, len(steps), step, args))

    def run():
        for _, _, step, args in sorted(steps, key=lambda item: item[:2]):
            step(*args)
        steps.clear()

    MOST = NY // 2
    core_copies = {}

    def slot_of(w, d, s):
        return d * MOST + s if d is not None else (1 - w) * MOST + MOST - 1

    def block_of(w, d, s):
        return at_y(d, hops(w, d) - s) if d is not None else y

    def multiply(w, d, s):
        block, slot = block_of(w, d, s), slot_of(w, d, s)
        parts[w, slot] = (
            jnp.dot(
                panel_rows[block],
                weights[w][...].reshape(-1, width),
                preferred_element_type=F32,
            )
            .astype(BF16)
            .reshape(2, 2, rows, width)
        )
        core_copies[w, d, s] = send(
            parts.at[w, slot, :, 1 - core],
            core_in.at[w, slot],
            core_send.at[w, slot],
            core_recv.at[w, slot],
            partner,
        )

    ring = {}
    seen = set()

    def here(w, d, s, j):
        if (w, d, s) not in seen:
            seen.add((w, d, s))
            core_copies[w, d, s].wait_recv()
        slot = slot_of(w, d, s)
        return parts[w, slot, zhs[j], core].astype(F32) + core_in[w, slot, zhs[j]].astype(F32)

    def ring_step(w, d, s, j):
        total = here(w, d, s, j)
        if s > 0:
            ring[w, d, j, s - 1].wait_recv()
            total = total + ring_in[w, d, j, s - 1].astype(F32)
        ring_out[w, d, j, s] = total.astype(BF16)
        ring[w, d, j, s] = send(
            ring_out.at[w, d, j, s],
            ring_in.at[w, d, j, s],
            ring_send.at[w, d, j, s],
            ring_recv.at[w, d, j, s],
            y_next[d],
        )

    near = {}
    far = {}

    def ring_end(w, j):
        total = here(w, None, 0, j)
        for d in (1 - w, w):
            last = hops(w, d) - 1
            ring[w, d, j, last].wait_recv()
            total = total + ring_in[w, d, j, last].astype(F32)
        if j == 0:
            pair_out[w] = total.astype(BF16)
            near[w, 0] = send(
                pair_out.at[w],
                relay_in.at[w, 0],
                relay_send.at[w, 0],
                relay_recv.at[w, 0],
                z_near[w],
            )
        else:
            own[w] = total

    def relay(w):
        near[w, 0].wait_recv()
        far[w, 0] = send(
            relay_in.at[w, 0], pair_in.at[w], pair_send.at[w], pair_recv.at[w], z_far[w]
        )

    for w, d in BOTH:
        for s in range(hops(w, d)):
            plan(3.5 * (s - 1) - 1.0, multiply, w, d, s)
            for j in range(2):
                plan(3.5 * s + 6.0 * j, ring_step, w, d, s, j)
    for w in range(2):
        plan(9.0, multiply, w, None, 0)
        plan(14.0, ring_end, w, 0)
        plan(17.0, relay, w)
        plan(20.0, ring_end, w, 1)
    run()
    for w in range(2):
        far[w, 0].wait_recv()
    gate = own[0] + pair_in[0].astype(F32)
    up = own[1] + pair_in[1].astype(F32)
    sigma = jax.nn.sigmoid(gate)
    upstream = hidden_ref[...].astype(F32)
    acts[0, y, zh, core] = (upstream * up * sigma * (1.0 + gate * (1.0 - sigma))).astype(BF16)
    acts[1, y, zh, core] = (upstream * gate * sigma).astype(BF16)

    turn = {}
    fwd = {}
    for w in range(2):
        near[w, 1] = send(
            acts.at[w, y, zh, core],
            relay_in.at[w, 1],
            relay_send.at[w, 1],
            relay_recv.at[w, 1],
            z_near[w],
        )

    def relay_act(w):
        near[w, 1].wait_recv()
        far[w, 1] = send(
            relay_in.at[w, 1],
            acts.at[w, y, z_from[w], core],
            swap_send.at[w],
            swap_recv.at[w],
            z_far[w],
        )

    def pass_on(w, d, j, s):
        here = acts.at[w, at_y(d, -s), zhs[j], core]
        if s > 0:
            turn[w, d, j, s - 1].wait_recv()
        if s < hops(w, d):
            turn[w, d, j, s] = send(
                here, here, turn_send.at[w, d, j, s], turn_recv.at[w, d, j, s], y_next[d]
            )
        if s > 0 or d == 0:
            fwd[w, d, j, s] = send(
                here, here, fwd_send.at[w, d, j, s], fwd_recv.at[w, d, j, s], partner
            )

    def arrive(w):
        far[w, 1].wait_recv()
        for d in range(2):
            pass_on(w, d, 0, 0)

    for w in range(2):
        for d in range(2):
            pass_on(w, d, 1, 0)
            for s in range(1, hops(w, d) + 1):
                plan(2.3 * s + 0.5 * w, pass_on, w, d, 1, s)
                plan((8.0, 9.0)[w] + 2.3 * s, pass_on, w, d, 0, s)
        plan(2.2, relay_act, w)
        plan((8.0, 9.0)[w], arrive, w)

    order = [lax.rem(dp + o, NX) for o in (NX - 1, 1, 2, 0)]
    slots = ((0, 2, 1, 3), (1, 2, 0, 3))
    dps = {}
    back = {}

    def gathered(w):
        for key, copy in fwd.items():
            if key[0] == w:
                copy.wait_recv()

    def dp_send_on(w, d, s, src):
        dps[w, d, s] = send(
            src, dp_in.at[w, d, s], dp_send.at[w, d, s], dp_recv.at[w, d, s], x_next[d]
        )

    def product(w, k):
        value = jnp.dot(
            panel_ref[order[k]],
            acts[w].reshape(-1, width),
            preferred_element_type=F32,
        ).astype(BF16)
        for d in range(2):
            local[w, k, d] = value[d * half : (d + 1) * half]
        if k < 2:
            dp_send_on(w, k, 0, local.at[w, k, k])

    def dp_step(w, d, s):
        dps[w, d, s - 1].wait_recv()
        total = local[w, slots[d][s], d].astype(F32) + dp_in[w, d, s - 1].astype(F32)
        if s < NX - 1:
            dp_out[w, d, s - 1] = total.astype(BF16)
            dp_send_on(w, d, s, dp_out.at[w, d, s - 1])
        else:
            outs[w][dp, d] = total.astype(BF16)
            back_on(w, d, 0)

    def back_on(w, d, s):
        if s > 0:
            back[w, d, s - 1].wait_recv()
        if s < NX - 1:
            at = lax.rem(dp + NX + (-s if d == 0 else s), NX)
            back[w, d, s] = send(
                outs[w].at[at, d],
                outs[w].at[at, d],
                back_send.at[w, d, s],
                back_recv.at[w, d, s],
                x_next[d],
            )

    starts = (18.5, 22.0)
    for w in range(2):
        plan(starts[w], gathered, w)
        for k in range(NX):
            plan(starts[w] + 0.1 + k, product, w, k)
        for d in range(2):
            for s in range(1, NX):
                plan(starts[w] + 1.5 + 4.8 * s, dp_step, w, d, s)
                plan(starts[w] + 1.5 + 4.8 * (NX - 1 + s), back_on, w, d, s)

    share = {}

    def share_step(o):
        block = lax.rem(col + o + 1, NC)
        total = lax.dot_general(
            gate_weight_ref[block], acts[0].reshape(-1, width), (((1,), (1,)), ((), ())),
            preferred_element_type=F32,
        ) + lax.dot_general(
            up_weight_ref[block], acts[1].reshape(-1, width), (((1,), (1,)), ((), ())),
            preferred_element_type=F32,
        )
        if o < NC - 1:
            share_out[o] = total.astype(BF16)
            share[o] = send(
                share_out.at[o], share_in.at[o], share_send.at[o], share_recv.at[o], peers[o]
            )
        else:
            share_own[...] = total

    def share_end():
        total = share_own[...]
        for o in range(NC - 1):
            share[o].wait_recv()
            total = total + share_in[o].astype(F32)
        input_out[...] = total.astype(BF16)

    for o in range(NC):
        plan(starts[1] + 5.0 + 2.4 * o, share_step, o)
    plan(starts[1] + 22.0, share_end)

    run()
    for copy in sent:
        copy.wait_send()


def main_call(tokens_t, hidden, gate_weight, up_weight):
    rows, width = hidden.shape
    features = gate_weight.shape[0]
    tokens = tokens_t.shape[1]
    part = features // NC
    half = features // NX // 2
    shape = (NY, 2, 2, rows, width)
    most = NY // 2
    dma = pltpu.SemaphoreType.DMA
    vm = pltpu.VMEM
    gate_sum, up_sum, input_sum = pl.pallas_call(
        main_kernel,
        out_shape=[jax.ShapeDtypeStruct((NX, 2, half, width), BF16)] * 2
        + [jax.ShapeDtypeStruct((part, tokens), BF16)],
        in_specs=[vmem()] * 4,
        out_specs=[vmem()] * 3,
        scratch_shapes=[
            vm((NC, part, tokens), BF16),
            vm((NY, tokens // NY, features), BF16),
            vm((2, 2 * most, 2, 2, rows, width), BF16),
            vm((2, 2, rows, width), BF16),
            vm((2, 2 * most, 2, rows, width), BF16),
            vm((2, 2, 2, most, rows, width), BF16),
            vm((2, 2, 2, most, rows, width), BF16),
            vm((2, rows, width), F32),
            vm((2, rows, width), BF16),
            vm((2, rows, width), BF16),
            vm((2, *shape), BF16),
            vm((2, NX, 2, half, width), BF16),
            vm((2, 2, NX - 2, half, width), BF16),
            vm((2, 2, NX - 1, half, width), BF16),
            vm((NC - 1, part, tokens), BF16),
            vm((NC - 1, part, tokens), BF16),
            vm((part, tokens), F32),
            dma,
            *[dma((NC - 1,))] * 2,
            *[dma((2, 2))] * 2,
            *[dma((2, 2 * most))] * 2,
            *[dma((2, 2, 2, most))] * 2,
            *[dma((2,))] * 2,
            *[dma((2,))] * 2,
            *[dma((2, 2, 2, most))] * 2,
            *[dma((2, 2, 2, most + 1))] * 2,
            *[dma((2, 2, NX - 1))] * 2,
            *[dma((2, 2, NX - 1))] * 2,
            *[dma((NC - 1,))] * 2,
        ],
        compiler_params=params(1),
        name="main",
    )(
        tokens_t,
        hidden,
        gate_weight.reshape(NC, part, width),
        up_weight.reshape(NC, part, width),
    )
    return input_sum.T, gate_sum.reshape(features, width), up_sum.reshape(features, width)


def body(tokens, hidden_grad, gate_weight, up_weight):
    return main_call(tokens.T, hidden_grad, gate_weight, up_weight)


def solution(mesh):
    return jax.shard_map(
        body,
        mesh=mesh,
        in_specs=(
            P("dp", ("row", "col")),
            P(("dp", "row"), "col"),
            P("row", "col"),
            P("row", "col"),
        ),
        out_specs=(P("dp", ("row", "col")), P("row", "col"), P("row", "col")),
        check_vma=False,
    )
```

```python
import jax
import jax.numpy as jnp
from jax import lax
from jax.experimental import pallas as pl
from jax.experimental.pallas import tpu as pltpu
from jax.sharding import PartitionSpec as P

MESH = pl.DeviceIdType.MESH
F32 = jnp.float32
BF16 = jnp.bfloat16
NY, NX, NC = 8, 4, 4


def remote(src, dst, send, recv, target):
    copy = pltpu.make_async_remote_copy(
        src_ref=src,
        dst_ref=dst,
        send_sem=send,
        recv_sem=recv,
        device_id=target,
        device_id_type=MESH,
    )
    copy.start()
    return copy


def greet(targets):
    barrier = pltpu.get_barrier_semaphore()
    for target in targets:
        pl.semaphore_signal(barrier, inc=1, device_id=target, device_id_type=MESH)
    pl.semaphore_wait(barrier, len(targets))


def vmem():
    return pl.BlockSpec(memory_space=pltpu.VMEM)


def params(collective_id):
    return pltpu.CompilerParams(collective_id=collective_id, has_side_effects=True)


def main_kernel(
    tokens_ref, hidden_ref, gate_weight_ref, up_weight_ref,
    gate_out, up_out, input_out,
    panel_ref, panel_rows, parts, relay_in,
    core_in, ring_out, ring_in, own, pair_out, pair_in, acts,
    local, dp_out, dp_in, share_out, share_in, share_own,
    own_sem, panel_send, panel_recv, relay_send, relay_recv,
    core_send, core_recv, ring_send, ring_recv, pair_send, pair_recv,
    swap_send, swap_recv, turn_send, turn_recv, fwd_send, fwd_recv,
    dp_send, dp_recv, back_send, back_recv, share_send, share_recv,
):
    row = lax.axis_index("row")
    dp = lax.axis_index("dp")
    col = lax.axis_index("col")
    y = lax.div(row, 4)
    core = lax.rem(row, 2)
    zh = lax.rem(lax.div(row, 2), 2)
    low = lax.rem(row, 4)
    y_next = (
        {"row": lax.rem(y + 1, NY) * 4 + low},
        {"row": lax.rem(y + NY - 1, NY) * 4 + low},
    )
    x_next = ({"dp": lax.rem(dp + 1, NX)}, {"dp": lax.rem(dp + NX - 1, NX)})
    partner = {"row": y * 4 + zh * 2 + (1 - core)}
    z = zh * NC + col

    def at_z(hops):
        there = lax.rem(z + 2 * NC + hops, 2 * NC)
        return {"row": y * 4 + lax.div(there, NC) * 2 + core, "col": lax.rem(there, NC)}

    z_near = (at_z(-1), at_z(1))
    z_far = (at_z(-3), at_z(3))
    z_from = (lax.div(lax.rem(z + 1, 2 * NC), NC), lax.div(lax.rem(z + 2 * NC - 1, 2 * NC), NC))
    peers = [{"col": lax.rem(col + o, NC)} for o in range(1, NC)]
    greet([*y_next, partner, *z_near, *z_far, *x_next, *peers])

    weights = (gate_weight_ref, up_weight_ref)
    outs = (gate_out, up_out)
    zhs = (1 - zh, zh)
    BOTH = ((0, 0), (0, 1), (1, 0), (1, 1))
    sent = []

    def send(*args):
        copy = remote(*args)
        sent.append(copy)
        return copy

    def hops(w, d):
        return NY // 2 if w == d else NY // 2 - 1

    def at_y(d, ahead):
        return lax.rem(y + NY + (ahead if d == 0 else -ahead), NY)

    half = local.shape[3]
    width = local.shape[4]
    rows = hidden_ref.shape[0]
    panels = [
        send(tokens_ref, panel_ref.at[col], panel_send.at[o], panel_recv.at[o], peers[o])
        for o in range(NC - 1)
    ]
    mine = pltpu.make_async_copy(tokens_ref, panel_ref.at[col], own_sem)
    mine.start()
    mine.wait()
    for copy in panels:
        copy.wait_recv()
    panel_rows[...] = (
        panel_ref[...].reshape(-1, panel_ref.shape[2]).T.reshape(panel_rows.shape)
    )

    steps = []

    def plan(time, step, *args):
        steps.append((time, len(steps), step, args))

    def run():
        for _, _, step, args in sorted(steps, key=lambda item: item[:2]):
            step(*args)
        steps.clear()

    MOST = NY // 2
    core_copies = {}

    def slot_of(w, d, s):
        return d * MOST + s if d is not None else (1 - w) * MOST + MOST - 1

    def block_of(w, d, s):
        return at_y(d, hops(w, d) - s) if d is not None else y

    def multiply(w, d, s):
        block, slot = block_of(w, d, s), slot_of(w, d, s)
        parts[w, slot] = (
            jnp.dot(
                panel_rows[block],
                weights[w][...].reshape(-1, width),
                preferred_element_type=F32,
            )
            .astype(BF16)
            .reshape(2, 2, rows, width)
        )
        core_copies[w, d, s] = send(
            parts.at[w, slot, :, 1 - core],
            core_in.at[w, slot],
            core_send.at[w, slot],
            core_recv.at[w, slot],
            partner,
        )

    ring = {}
    seen = set()

    def here(w, d, s, j):
        if (w, d, s) not in seen:
            seen.add((w, d, s))
            core_copies[w, d, s].wait_recv()
        slot = slot_of(w, d, s)
        return parts[w, slot, zhs[j], core].astype(F32) + core_in[w, slot, zhs[j]].astype(F32)

    def ring_step(w, d, s, j):
        total = here(w, d, s, j)
        if s > 0:
            ring[w, d, j, s - 1].wait_recv()
            total = total + ring_in[w, d, j, s - 1].astype(F32)
        ring_out[w, d, j, s] = total.astype(BF16)
        ring[w, d, j, s] = send(
            ring_out.at[w, d, j, s],
            ring_in.at[w, d, j, s],
            ring_send.at[w, d, j, s],
            ring_recv.at[w, d, j, s],
            y_next[d],
        )

    near = {}
    far = {}

    def ring_end(w, j):
        total = here(w, None, 0, j)
        for d in (1 - w, w):
            last = hops(w, d) - 1
            ring[w, d, j, last].wait_recv()
            total = total + ring_in[w, d, j, last].astype(F32)
        if j == 0:
            pair_out[w] = total.astype(BF16)
            near[w, 0] = send(
                pair_out.at[w],
                relay_in.at[w, 0],
                relay_send.at[w, 0],
                relay_recv.at[w, 0],
                z_near[w],
            )
        else:
            own[w] = total

    def relay(w):
        near[w, 0].wait_recv()
        far[w, 0] = send(
            relay_in.at[w, 0], pair_in.at[w], pair_send.at[w], pair_recv.at[w], z_far[w]
        )

    for w, d in BOTH:
        for s in range(hops(w, d)):
            plan(3.5 * (s - 1) - 1.0, multiply, w, d, s)
            for j in range(2):
                plan(3.5 * s + 6.0 * j, ring_step, w, d, s, j)
    for w in range(2):
        plan(9.0, multiply, w, None, 0)
        plan(14.0, ring_end, w, 0)
        plan(17.0, relay, w)
        plan(20.0, ring_end, w, 1)
    run()
    for w in range(2):
        far[w, 0].wait_recv()
    gate = own[0] + pair_in[0].astype(F32)
    up = own[1] + pair_in[1].astype(F32)
    sigma = jax.nn.sigmoid(gate)
    upstream = hidden_ref[...].astype(F32)
    acts[0, y, zh, core] = (upstream * up * sigma * (1.0 + gate * (1.0 - sigma))).astype(BF16)
    acts[1, y, zh, core] = (upstream * gate * sigma).astype(BF16)

    turn = {}
    fwd = {}
    for w in range(2):
        near[w, 1] = send(
            acts.at[w, y, zh, core],
            relay_in.at[w, 1],
            relay_send.at[w, 1],
            relay_recv.at[w, 1],
            z_near[w],
        )

    def relay_act(w):
        near[w, 1].wait_recv()
        far[w, 1] = send(
            relay_in.at[w, 1],
            acts.at[w, y, z_from[w], core],
            swap_send.at[w],
            swap_recv.at[w],
            z_far[w],
        )

    def pass_on(w, d, j, s):
        here = acts.at[w, at_y(d, -s), zhs[j], core]
        if s > 0:
            turn[w, d, j, s - 1].wait_recv()
        if s < hops(w, d):
            turn[w, d, j, s] = send(
                here, here, turn_send.at[w, d, j, s], turn_recv.at[w, d, j, s], y_next[d]
            )
        if s > 0 or d == 0:
            fwd[w, d, j, s] = send(
                here, here, fwd_send.at[w, d, j, s], fwd_recv.at[w, d, j, s], partner
            )

    def arrive(w):
        far[w, 1].wait_recv()
        for d in range(2):
            pass_on(w, d, 0, 0)

    for w in range(2):
        for d in range(2):
            plan(4.0 * w, pass_on, w, d, 1, 0)
            for s in range(1, hops(w, d) + 1):
                plan(2.3 * s + 4.1 * w, pass_on, w, d, 1, s)
                plan((8.0, 12.5)[w] + 2.3 * s, pass_on, w, d, 0, s)
        plan(2.2, relay_act, w)
        plan((8.0, 12.5)[w], arrive, w)

    order = [lax.rem(dp + o, NX) for o in (NX - 1, 1, 2, 0)]
    slots = ((0, 2, 1, 3), (1, 2, 0, 3))
    dps = {}
    back = {}

    def gathered(w):
        for key, copy in fwd.items():
            if key[0] == w:
                copy.wait_recv()

    def dp_send_on(w, d, s, src):
        dps[w, d, s] = send(
            src, dp_in.at[w, d, s], dp_send.at[w, d, s], dp_recv.at[w, d, s], x_next[d]
        )

    def product(w, k):
        value = jnp.dot(
            panel_ref[order[k]],
            acts[w].reshape(-1, width),
            preferred_element_type=F32,
        ).astype(BF16)
        for d in range(2):
            local[w, k, d] = value[d * half : (d + 1) * half]
        if k < 2:
            dp_send_on(w, k, 0, local.at[w, k, k])

    def dp_step(w, d, s):
        dps[w, d, s - 1].wait_recv()
        total = local[w, slots[d][s], d].astype(F32) + dp_in[w, d, s - 1].astype(F32)
        if s < NX - 1:
            dp_out[w, d, s - 1] = total.astype(BF16)
            dp_send_on(w, d, s, dp_out.at[w, d, s - 1])
        else:
            outs[w][dp, d] = total.astype(BF16)
            back_on(w, d, 0)

    def back_on(w, d, s):
        if s > 0:
            back[w, d, s - 1].wait_recv()
        if s < NX - 1:
            at = lax.rem(dp + NX + (-s if d == 0 else s), NX)
            back[w, d, s] = send(
                outs[w].at[at, d],
                outs[w].at[at, d],
                back_send.at[w, d, s],
                back_recv.at[w, d, s],
                x_next[d],
            )

    starts = (18.5, 23.0)
    for w in range(2):
        plan(starts[w], gathered, w)
        for k in range(NX):
            plan(starts[w] + 0.1 + k, product, w, k)
        for d in range(2):
            for s in range(1, NX):
                plan(starts[w] + 1.5 + 4.8 * s, dp_step, w, d, s)
                plan(starts[w] + 1.5 + 4.8 * (NX - 1 + s), back_on, w, d, s)

    share = {}

    def share_step(o):
        block = lax.rem(col + o + 1, NC)
        total = lax.dot_general(
            gate_weight_ref[block], acts[0].reshape(-1, width), (((1,), (1,)), ((), ())),
            preferred_element_type=F32,
        ) + lax.dot_general(
            up_weight_ref[block], acts[1].reshape(-1, width), (((1,), (1,)), ((), ())),
            preferred_element_type=F32,
        )
        if o < NC - 1:
            share_out[o] = total.astype(BF16)
            share[o] = send(
                share_out.at[o], share_in.at[o], share_send.at[o], share_recv.at[o], peers[o]
            )
        else:
            share_own[...] = total

    def share_end():
        total = share_own[...]
        for o in range(NC - 1):
            share[o].wait_recv()
            total = total + share_in[o].astype(F32)
        input_out[...] = total.astype(BF16)

    for o in range(NC):
        plan(starts[1] + 5.0 + 2.4 * o, share_step, o)
    plan(starts[1] + 22.0, share_end)

    run()
    for copy in sent:
        copy.wait_send()


def settle_kernel(*refs):
    ins, outs, bufs, (in_sem, out_sem) = refs[:3], refs[3:6], refs[6:9], refs[9:]
    pieces = [(i, k) for k in range(NX) for i in range(3)]
    arriving = []
    for n, (i, k) in enumerate(pieces):
        arriving.append(pltpu.make_async_copy(ins[i].at[k], bufs[i].at[k], in_sem.at[n]))
        arriving[-1].start()
    leaving = []
    for n, (i, k) in enumerate(pieces):
        arriving[n].wait()
        leaving.append(pltpu.make_async_copy(bufs[i].at[k], outs[i].at[k], out_sem.at[n]))
        leaving[-1].start()
    for copy in leaving:
        copy.wait()


def settle(*arrays):
    return pl.pallas_call(
        settle_kernel,
        out_shape=[jax.ShapeDtypeStruct(a.shape, a.dtype) for a in arrays],
        in_specs=[pl.BlockSpec(memory_space=pl.ANY)] * 3,
        out_specs=[pl.BlockSpec(memory_space=pl.ANY)] * 3,
        scratch_shapes=[pltpu.VMEM(a.shape, a.dtype) for a in arrays]
        + [pltpu.SemaphoreType.DMA((3 * NX,))] * 2,
        name="settle",
    )(*arrays)


def main_call(tokens_t, hidden, gate_weight, up_weight):
    rows, width = hidden.shape
    features = gate_weight.shape[0]
    tokens = tokens_t.shape[1]
    part = features // NC
    half = features // NX // 2
    shape = (NY, 2, 2, rows, width)
    most = NY // 2
    dma = pltpu.SemaphoreType.DMA
    vm = pltpu.VMEM
    gate_sum, up_sum, input_sum = pl.pallas_call(
        main_kernel,
        out_shape=[jax.ShapeDtypeStruct((NX, 2, half, width), BF16)] * 2
        + [jax.ShapeDtypeStruct((part, tokens), BF16)],
        in_specs=[vmem()] * 4,
        out_specs=[vmem()] * 3,
        scratch_shapes=[
            vm((NC, part, tokens), BF16),
            vm((NY, tokens // NY, features), BF16),
            vm((2, 2 * most, 2, 2, rows, width), BF16),
            vm((2, 2, rows, width), BF16),
            vm((2, 2 * most, 2, rows, width), BF16),
            vm((2, 2, 2, most, rows, width), BF16),
            vm((2, 2, 2, most, rows, width), BF16),
            vm((2, rows, width), F32),
            vm((2, rows, width), BF16),
            vm((2, rows, width), BF16),
            vm((2, *shape), BF16),
            vm((2, NX, 2, half, width), BF16),
            vm((2, 2, NX - 2, half, width), BF16),
            vm((2, 2, NX - 1, half, width), BF16),
            vm((NC - 1, part, tokens), BF16),
            vm((NC - 1, part, tokens), BF16),
            vm((part, tokens), F32),
            dma,
            *[dma((NC - 1,))] * 2,
            *[dma((2, 2))] * 2,
            *[dma((2, 2 * most))] * 2,
            *[dma((2, 2, 2, most))] * 2,
            *[dma((2,))] * 2,
            *[dma((2,))] * 2,
            *[dma((2, 2, 2, most))] * 2,
            *[dma((2, 2, 2, most + 1))] * 2,
            *[dma((2, 2, NX - 1))] * 2,
            *[dma((2, 2, NX - 1))] * 2,
            *[dma((NC - 1,))] * 2,
        ],
        compiler_params=params(1),
        name="main",
    )(
        tokens_t,
        hidden,
        gate_weight.reshape(NC, part, width),
        up_weight.reshape(NC, part, width),
    )
    gate_sum, up_sum, input_sum = settle(
        gate_sum, up_sum, input_sum.reshape(NX, part // NX, tokens)
    )
    return (
        input_sum.reshape(part, tokens).T,
        gate_sum.reshape(features, width),
        up_sum.reshape(features, width),
    )


def body(tokens, hidden_grad, gate_weight, up_weight):
    return main_call(tokens.T, hidden_grad, gate_weight, up_weight)


def solution(mesh):
    return jax.shard_map(
        body,
        mesh=mesh,
        in_specs=(
            P("dp", ("row", "col")),
            P(("dp", "row"), "col"),
            P("row", "col"),
            P("row", "col"),
        ),
        out_specs=(P("dp", ("row", "col")), P("row", "col"), P("row", "col")),
        check_vma=False,
    )
```
